32 devices in a mesh: gx: 4 (over y, x), gy: 2 (over core), gz: 4 (over z).
Axes of the slice: x: 2, y: 2, z: 4, core: 2. Of those that a mesh axis runs over, the one named last changes fastest.
Arguments:
- panel: float32 [4, 2, 16, 256, 256], P('gx', 'gy', 'gz'), may hold values from -120 to 120
- tiles: float32 [4, 2, 16, 10, 256, 256], P('gx', 'gy', 'gz'), may hold values from -0.125 to 0.125
- codes: int32 [4, 2, 16, 10], P('gx', 'gy', 'gz'), may hold values from 0 to 26, as said below
Outputs:
- bands: float32 [4, 2, 16, 256, 256], P('gx', 'gy', 'gz')
- factor: float32 [256, 256], replicated
The draws below stay inside these ranges and needn't reach their ends.
Inputs may be any that keep to these rules, and one draw needn't show every extreme that they name: Slot 0 of every element holds 13, the element itself; the other 9 slots of an element hold distinct codes other than 13.
All inputs are finite; a program needn't handle non-finite values.
Results may differ from the reference program's by a relative error of at most 0.0003.
Values sent between devices are 32-bit elements; how exact they have to be, the bound alone decides.
A program may use at most 128 MiB of HBM per device.

```python
import math
import jax
import jax.numpy as jnp
from jax import lax

BASIS_PER_ELEM = 256
BAND_COUNT = 256
TILE_SLOTS = 10
ELEMENTS_X = 4
ELEMENTS_Y = 2
ELEMENTS_Z = 16


def draw_codes(key, part):
    grand_total = ELEMENTS_X * ELEMENTS_Y * ELEMENTS_Z

    def element_cell(index):
        order = jax.random.permutation(jax.random.fold_in(key, index), 26).astype(jnp.int32)
        others = order[:TILE_SLOTS - 1]
        others = others + (others >= 13).astype(jnp.int32)
        return jnp.concatenate([jnp.full((1,), 13, jnp.int32), others])
    return jax.vmap(element_cell)(jnp.arange(grand_total, dtype=jnp.int32)).reshape(ELEMENTS_X, ELEMENTS_Y, ELEMENTS_Z, TILE_SLOTS)


def draw_panel(key, part):
    panel_random_key = jax.random.split(jax.random.fold_in(key, 7), 5)
    array_shape = (ELEMENTS_X, ELEMENTS_Y, ELEMENTS_Z, BASIS_PER_ELEM, BAND_COUNT)
    common_shape = (ELEMENTS_X, ELEMENTS_Y, ELEMENTS_Z, BASIS_PER_ELEM, 4)
    base = jnp.clip(jax.random.normal(panel_random_key[2], array_shape, jnp.float32), -4.0, 4.0)
    shared = jnp.clip(jax.random.normal(panel_random_key[3], common_shape, jnp.float32), -4.0, 4.0)
    element_scale_factor = jnp.exp(jax.random.uniform(panel_random_key[0], (ELEMENTS_X, ELEMENTS_Y, ELEMENTS_Z, 1, 1), jnp.float32) * math.log(10.0))
    mixing = jax.random.uniform(panel_random_key[4], (4, BAND_COUNT), jnp.float32, -1.5, 1.5)
    combined = base
    for component in range(4):
        combined = combined + 0.3 * shared[..., component:component + 1] * mixing[component]
    combined = combined / 2.8
    band_scale = 0.3 * jnp.exp(jax.random.uniform(panel_random_key[1], (1, 1, 1, 1, BAND_COUNT), jnp.float32) * math.log(10.0))
    return combined * element_scale_factor * band_scale


def levels(own_key, dims, shards, low, top_value):
    def one(axis_at, parts):
        draws = jax.random.uniform(jax.random.fold_in(jax.random.fold_in(own_key, 6), axis_at), (parts,), jnp.float32, low / len(shards), top_value / len(shards))
        return jnp.repeat(jnp.exp(draws), dims[axis_at] // parts).reshape((-1,) + (1,) * (len(dims) - axis_at - 1))

    factor_of = one(*shards[0])
    for cut in shards[1:]:
        factor_of = factor_of * one(*cut)
    return factor_of


def normal_values(rng, shape, scale, limit, pieces=(), kind=jnp.bfloat16):
    values = jax.random.normal(rng, shape, jnp.float32) * scale
    if len(pieces) > 0:
        values = levels(rng, shape, pieces, -0.22, 0.18) * values
    return jnp.clip(values, min=-limit, max=limit).astype(kind)


def setup_inputs(seed: int = 0) -> dict:
    key_list = jax.random.split(jax.random.key(seed), 4)
    return {
        "panel": draw_panel(jax.random.fold_in(key_list[3], 71), 0),
        "tiles": normal_values(key_list[1], (ELEMENTS_X, ELEMENTS_Y, ELEMENTS_Z, TILE_SLOTS, BASIS_PER_ELEM, BASIS_PER_ELEM), (BASIS_PER_ELEM * TILE_SLOTS) ** -0.5, 0.125, ((0, 4), (1, 2), (2, 4)), jnp.float32),
        "codes": draw_codes(jax.random.fold_in(key_list[3], 71), 0),
    }


def reference(panel, tiles, codes):
    grid_y = panel.shape[1]
    grid_z = panel.shape[2]
    grand_total = panel.shape[0] * grid_y * grid_z
    padded = jnp.pad(panel, ((1, 1), (1, 1), (1, 1), (0, 0), (0, 0)))
    basis = panel.shape[3]
    width = panel.shape[4]

    def window(first, second, third):
        zero = jnp.zeros((), jnp.int32)
        piece = lax.dynamic_slice(padded, (first.astype(jnp.int32), second.astype(jnp.int32), third.astype(jnp.int32), zero, zero), (1, 1, 1, basis, width))
        return piece[0, 0, 0]

    def element_cell(flat):
        x_index = flat // (grid_y * grid_z)
        y_index = flat // grid_z % grid_y
        z_index = flat % grid_z
        slot_codes = codes[x_index, y_index, z_index]
        windows = jax.vmap(lambda c: window(x_index + c // 9, y_index + c // 3 % 3, z_index + c % 3))(slot_codes)
        applied = jnp.einsum('kab,kbc->ac', tiles[x_index, y_index, z_index], windows, precision=lax.Precision.HIGHEST)
        return applied - 0.5 * panel[x_index, y_index, z_index]
    filtered = lax.map(element_cell, jnp.arange(grand_total, dtype=jnp.int32))
    flat_rows = filtered.reshape(-1, width)
    gram = jnp.dot(flat_rows.T, flat_rows, precision=lax.Precision.HIGHEST) / flat_rows.shape[0]
    lower = jnp.linalg.cholesky(gram)
    inverse = lax.linalg.triangular_solve(lower, jnp.eye(width, dtype=gram.dtype), left_side=True, lower=True)
    bands = jnp.dot(flat_rows, inverse.T, precision=lax.Precision.HIGHEST).reshape(panel.shape)
    return (bands, lower.T)
```

```python
import functools
import jax
import jax.numpy as jnp
from jax import lax
from jax.experimental import pallas as pl
from jax.experimental.pallas import tpu as pltpu
from jax.sharding import PartitionSpec as P

MESH = pl.DeviceIdType.MESH
PIECES = 2
BLOCK = 32


def split(value):
    high = value.astype(jnp.bfloat16)
    low = (value - high.astype(jnp.float32)).astype(jnp.bfloat16)
    return high, low


def product(left, right, dims):
    dot = functools.partial(
        lax.dot_general, dimension_numbers=(dims, ((), ())), preferred_element_type=jnp.float32
    )
    return dot(left[0], right[0]) + (dot(left[0], right[1]) + dot(left[1], right[0]))


def halo_kernel(sizes, panel_ref, halo_ref, x_sent, z_sent, y_sent, arrived):
    nx, ny, nz = sizes
    ix, iy, iz = (lax.axis_index(a) for a in ("gx", "gy", "gz"))
    depth, rows = panel_ref.shape[2], panel_ref.shape[3]
    part = rows // PIECES
    squared = nx == 4
    below, above = iz > 0, iz < nz - 1
    front, back = iy > 0, iy < ny - 1

    if squared:
        across = ix + 1 - 2 * lax.rem(ix, 2)
        beside = lax.rem(ix + 2, 4)
        slot_a, valid_a = 2 * lax.rem(ix + 1, 2), None
        slot_b, valid_b = 2 - slot_a, (ix == 1) | (ix == 2)
        relays = (ix == 0) | (ix == 3)
        partners_x = ((across, None), (beside, None))
    else:
        slot_a, valid_a = jnp.int32(0), ix > 0
        slot_b, valid_b = jnp.int32(2), ix < nx - 1
        partners_x = ((ix - 1, valid_a), (ix + 1, valid_b))

    def when(cond, action):
        if cond is None:
            action()
        else:
            pl.when(cond)(action)

    def both(*conds):
        conds = [c for c in conds if c is not None]
        return functools.reduce(jnp.logical_and, conds) if conds else None

    barrier = pltpu.get_barrier_semaphore()
    partners = (
        [("gx", d, c) for d, c in partners_x]
        + [("gz", iz - 1, below), ("gz", iz + 1, above)]
        + [("gy", iy - 1, front), ("gy", iy + 1, back)]
    )
    total = jnp.int32(0)
    for axis, device, cond in partners:
        when(
            cond,
            lambda axis=axis, device=device: pl.semaphore_signal(
                barrier, inc=1, device_id={axis: device}, device_id_type=MESH
            ),
        )
        total = total + (1 if cond is None else cond.astype(jnp.int32))
    pl.semaphore_wait(barrier, total)

    sends = []

    def own(z, c):
        return panel_ref.at[0, 0, z, pl.ds(c * part, part)]

    def cell(a, b, z, c):
        return halo_ref.at[a, b, z, pl.ds(c * part, part)]

    def send(cond, source, target, sem, slot, axis, device):
        a, b, z, c = slot

        def start():
            pltpu.make_async_remote_copy(
                src_ref=source,
                dst_ref=target,
                send_sem=sem,
                recv_sem=arrived.at[a, b, z, c],
                device_id={axis: device},
                device_id_type=MESH,
            ).start()

        when(cond, start)
        sends.append((cond, source, sem))

    def wait(cond, a, b, z, c):
        ref = cell(a, b, z, c)
        when(cond, lambda: pltpu.make_async_copy(ref, ref, arrived.at[a, b, z, c]).wait())

    def send_y(cond, source, a, z, c):
        send(both(cond, front), source, cell(a, 2, z, c), y_sent.at[0, a, z, c],
             (a, 2, z, c), "gy", iy - 1)
        send(both(cond, back), source, cell(a, 0, z, c), y_sent.at[1, a, z, c],
             (a, 0, z, c), "gy", iy + 1)

    def send_z(cond, source, a, z, c):
        if z == 0:
            send(both(cond, below), source, cell(a, 1, depth + 1, c), z_sent.at[0, a, c],
                 (a, 1, depth + 1, c), "gz", iz - 1)
        if z == depth - 1:
            send(both(cond, above), source, cell(a, 1, 0, c), z_sent.at[1, a, c],
                 (a, 1, 0, c), "gz", iz + 1)

    order = [0, depth - 1] + list(range(1, depth - 1)) if depth > 1 else [0]
    for z in order:
        for c in range(PIECES):
            if squared:
                target = 2 * lax.rem(ix, 2)
                send(None, own(z, c), cell(target, 1, z + 1, c), x_sent.at[0, z, c],
                     (target, 1, z + 1, c), "gx", across)
            else:
                send(valid_a, own(z, c), cell(2, 1, z + 1, c), x_sent.at[0, z, c],
                     (2, 1, z + 1, c), "gx", ix - 1)
                send(valid_b, own(z, c), cell(0, 1, z + 1, c), x_sent.at[1, z, c],
                     (0, 1, z + 1, c), "gx", ix + 1)
            send_z(None, own(z, c), 1, z, c)
    for z in order:
        for c in range(PIECES):
            send_y(None, own(z, c), 1, z + 1, c)

    def arrive(cond, a, z, c, relay=False):
        wait(cond, a, 1, z + 1, c)
        if relay and squared:
            target = 2 - a
            send(relays, cell(a, 1, z + 1, c), cell(target, 1, z + 1, c), x_sent.at[1, z, c],
                 (target, 1, z + 1, c), "gx", beside)
        send_z(cond, cell(a, 1, z + 1, c), a, z, c)
        send_y(cond, cell(a, 1, z + 1, c), a, z + 1, c)

    def arrive_z(cond, a):
        for side, slot in ((below, 0), (above, depth + 1)):
            for c in range(PIECES):
                ok = both(cond, side)
                wait(ok, a, 1, slot, c)
                send_y(ok, cell(a, 1, slot, c), a, slot, c)

    steps = [(k, c) for k in order for c in range(PIECES)]
    for at in range(len(steps) + 1):
        if at < len(steps):
            arrive(valid_a, slot_a, *steps[at], relay=True)
        if at >= 1:
            arrive(valid_b, slot_b, *steps[at - 1])
        if at == len(steps) // 2:
            arrive_z(None, 1)
        if at == len(steps) - 1:
            arrive_z(valid_a, slot_a)
    arrive_z(valid_b, slot_b)

    for b, side in ((0, front), (2, back)):
        for a, cond in ((1, None), (slot_a, valid_a), (slot_b, valid_b)):
            for z in range(depth + 2):
                edge = below if z == 0 else above if z == depth + 1 else None
                for c in range(PIECES):
                    wait(both(cond, edge, side), a, b, z, c)
    for cond, source, sem in sends:
        when(cond, lambda source=source, sem=sem: pltpu.make_async_copy(source, source, sem).wait())


def exchange_halo(panel, sizes):
    depth, rows, width = panel.shape[2:]
    return pl.pallas_call(
        functools.partial(halo_kernel, sizes),
        out_shape=jax.ShapeDtypeStruct((3, 3, depth + 2, rows, width), panel.dtype),
        in_specs=[pl.BlockSpec(memory_space=pl.ANY)],
        out_specs=pl.BlockSpec(memory_space=pl.ANY),
        scratch_shapes=[
            pltpu.SemaphoreType.DMA((2, depth, PIECES)),
            pltpu.SemaphoreType.DMA((2, 3, PIECES)),
            pltpu.SemaphoreType.DMA((2, 3, depth + 2, PIECES)),
            pltpu.SemaphoreType.DMA((3, 3, depth + 2, PIECES)),
        ],
        compiler_params=pltpu.CompilerParams(collective_id=0, has_side_effects=True),
        name="halo",
    )(panel)


def filter_kernel(sizes, codes_ref, panel_ref, tiles_ref, halo_ref, rows_ref, gram_ref,
                  tile_buf, window_buf, own_buf, tile_sem, window_sem, own_sem):
    nx, ny, nz = sizes
    ix, iy, iz = (lax.axis_index(a) for a in ("gx", "gy", "gz"))
    depth, slots = tiles_ref.shape[2], tiles_ref.shape[3]
    own = pltpu.make_async_copy(panel_ref.at[0, 0], own_buf, own_sem)
    own.start()

    def place(e, s):
        code = codes_ref[0, 0, e, s]
        a = code // 9
        b = lax.rem(code // 3, 3)
        z = e + lax.rem(code, 3)
        x_at, y_at, z_at = ix + a - 1, iy + b - 1, iz * depth + z - 1
        inside = ((x_at >= 0) & (x_at < nx) & (y_at >= 0) & (y_at < ny)
                  & (z_at >= 0) & (z_at < nz * depth))
        local = (a == 1) & (b == 1) & (z >= 1) & (z <= depth)
        return a, b, z, inside, local

    for e in range(depth):
        pltpu.make_async_copy(tiles_ref.at[0, 0, e], tile_buf.at[e], tile_sem.at[e]).start()

        def fetch(s, carry, e=e):
            a, b, z, inside, local = place(e, s)
            target, sem = window_buf.at[e, s], window_sem.at[e, s]

            @pl.when(inside & local)
            def _():
                pltpu.make_async_copy(panel_ref.at[0, 0, z - 1], target, sem).start()

            @pl.when(inside & jnp.logical_not(local))
            def _():
                pltpu.make_async_copy(halo_ref.at[a, b, z], target, sem).start()

            @pl.when(jnp.logical_not(inside))
            def _():
                window_buf[e, s] = jnp.zeros(window_buf.shape[2:], window_buf.dtype)

            return carry

        lax.fori_loop(0, slots, fetch, 0)
    own.wait()
    for e in range(depth):
        pltpu.make_async_copy(tiles_ref.at[0, 0, e], tile_buf.at[e], tile_sem.at[e]).wait()

        def apply(s, total, e=e):
            inside = place(e, s)[3]

            @pl.when(inside)
            def _():
                pltpu.make_async_copy(
                    window_buf.at[e, s], window_buf.at[e, s], window_sem.at[e, s]
                ).wait()

            return total + product(
                split(tile_buf[e, s]), split(window_buf[e, s]), ((1,), (0,))
            )

        filtered = lax.fori_loop(0, slots, apply, -0.5 * own_buf[e], unroll=2)
        rows_ref[e] = filtered
        pieces = split(filtered)
        term = product(pieces, pieces, ((0,), (0,)))
        gram_ref[...] = term if e == 0 else gram_ref[...] + term


def apply_filter(codes, panel, tiles, halo, sizes):
    depth, slots, rows, width = tiles.shape[2], tiles.shape[3], panel.shape[3], panel.shape[4]
    hbm = pl.BlockSpec(memory_space=pl.ANY)
    vmem = pl.BlockSpec(memory_space=pltpu.VMEM)
    return pl.pallas_call(
        functools.partial(filter_kernel, sizes),
        out_shape=(
            jax.ShapeDtypeStruct((depth, rows, width), jnp.float32),
            jax.ShapeDtypeStruct((width, width), jnp.float32),
        ),
        in_specs=[pl.BlockSpec(memory_space=pltpu.SMEM), hbm, hbm, hbm],
        out_specs=(vmem, vmem),
        scratch_shapes=[
            pltpu.VMEM((depth, slots, rows, rows), jnp.float32),
            pltpu.VMEM((depth, slots, rows, width), jnp.float32),
            pltpu.VMEM((depth, rows, width), jnp.float32),
            pltpu.SemaphoreType.DMA((depth,)),
            pltpu.SemaphoreType.DMA((depth, slots)),
            pltpu.SemaphoreType.DMA,
        ],
        compiler_params=pltpu.CompilerParams(vmem_limit_bytes=48 << 20),
        name="filter",
    )(codes, panel, tiles, halo)


def sum_kernel(sizes, gram_ref, out_ref, own, from_y, part_y, from_x, from_z, full,
               local_sem, y_send, y_recv, x_send, x_recv, z_send, z_recv,
               gx_send, gx_recv, gy_send, gy_recv):
    nx, ny, nz = sizes
    ix, iy, iz = (lax.axis_index(a) for a in ("gx", "gy", "gz"))
    rows_y = gram_ref.shape[0] // ny
    rows_x = rows_y // nx
    barrier = pltpu.get_barrier_semaphore()
    peers = {
        axis: [lax.rem(at + d, n) for d in range(1, n)]
        for axis, at, n in (("gx", ix, nx), ("gy", iy, ny), ("gz", iz, nz))
    }
    for axis, group in peers.items():
        for peer in group:
            pl.semaphore_signal(barrier, inc=1, device_id={axis: peer}, device_id_type=MESH)
    pl.semaphore_wait(barrier, nx + ny + nz - 3)

    def copy(source, target, send_sem, recv_sem, axis, peer):
        remote = pltpu.make_async_remote_copy(
            src_ref=source, dst_ref=target, send_sem=send_sem, recv_sem=recv_sem,
            device_id={axis: peer}, device_id_type=MESH,
        )
        remote.start()
        return remote

    def finish(copies):
        for remote in copies:
            remote.wait()

    def block(ref, at, count):
        return ref.at[pl.ds(pl.multiple_of(at * count, count), count)]

    finish([
        copy(block(gram_ref, peer, rows_y), from_y.at[d], y_send.at[d], y_recv.at[d], "gy", peer)
        for d, peer in enumerate(peers["gy"])
    ])
    total = gram_ref[pl.ds(pl.multiple_of(iy * rows_y, rows_y), rows_y), :]
    for d in range(ny - 1):
        total = total + from_y[d]
    part_y[...] = total
    finish([
        copy(block(part_y, peer, rows_x), from_x.at[d], x_send.at[d], x_recv.at[d], "gx", peer)
        for d, peer in enumerate(peers["gx"])
    ])
    total = part_y[pl.ds(pl.multiple_of(ix * rows_x, rows_x), rows_x), :]
    for d in range(nx - 1):
        total = total + from_x[d]
    from_z[pl.ds(iz, 1)] = total[None]
    started = [
        copy(from_z.at[iz], from_z.at[iz], z_send.at[d], z_recv.at[iz], "gz", peer)
        for d, peer in enumerate(peers["gz"])
    ]
    for remote in started:
        remote.wait_send()
    for peer in peers["gz"]:
        ref = from_z.at[peer]
        pltpu.make_async_copy(ref, ref, z_recv.at[peer]).wait()
    total = from_z[0]
    for d in range(1, nz):
        total = total + from_z[d]
    mine = iy * nx + ix
    full[pl.ds(pl.multiple_of(mine * rows_x, rows_x), rows_x), :] = total
    started = [
        copy(block(full, mine, rows_x), block(full, mine, rows_x), gx_send.at[d], gx_recv.at[ix],
             "gx", peer)
        for d, peer in enumerate(peers["gx"])
    ]
    for remote in started:
        remote.wait_send()
    for peer in peers["gx"]:
        ref = block(full, iy * nx + peer, rows_x)
        pltpu.make_async_copy(ref, ref, gx_recv.at[peer]).wait()
    started = [
        copy(block(full, iy, rows_y), block(full, iy, rows_y), gy_send.at[d], gy_recv.at[iy],
             "gy", peer)
        for d, peer in enumerate(peers["gy"])
    ]
    for remote in started:
        remote.wait_send()
    for peer in peers["gy"]:
        ref = block(full, peer, rows_y)
        pltpu.make_async_copy(ref, ref, gy_recv.at[peer]).wait()
    out_ref[...] = full[...]


def sum_gram(gram, sizes):
    nx, ny, nz = sizes
    size = gram.shape[0]
    rows_y = size // ny
    rows_x = rows_y // nx
    vmem = pl.BlockSpec(memory_space=pltpu.VMEM)
    dma = pltpu.SemaphoreType.DMA
    return pl.pallas_call(
        functools.partial(sum_kernel, sizes),
        out_shape=jax.ShapeDtypeStruct(gram.shape, gram.dtype),
        in_specs=[vmem],
        out_specs=vmem,
        scratch_shapes=[
            pltpu.VMEM((8, 128), jnp.float32),
            pltpu.VMEM((max(ny - 1, 1), rows_y, size), jnp.float32),
            pltpu.VMEM((rows_y, size), jnp.float32),
            pltpu.VMEM((max(nx - 1, 1), rows_x, size), jnp.float32),
            pltpu.VMEM((nz, rows_x, size), jnp.float32),
            pltpu.VMEM((size, size), jnp.float32),
            dma,
            dma((ny,)), dma((ny,)), dma((nx,)), dma((nx,)), dma((nz,)), dma((nz,)),
            dma((nx,)), dma((nx,)), dma((ny,)), dma((ny,)),
        ],
        compiler_params=pltpu.CompilerParams(collective_id=1, has_side_effects=True),
        name="sum",
    )(gram)


def factor_kernel(row_total, gram_ref, rows_ref, bands_ref, factor_ref, left, right, inverse):
    size = gram_ref.shape[0]
    exact = functools.partial(
        lax.dot_general, preferred_element_type=jnp.float32, precision=lax.Precision.HIGHEST
    )
    left[...] = gram_ref[...] / row_total
    right[...] = (
        lax.broadcasted_iota(jnp.int32, (size, size), 0)
        == lax.broadcasted_iota(jnp.int32, (size, size), 1)
    ).astype(jnp.float32)
    row_at = lax.broadcasted_iota(jnp.int32, (BLOCK, BLOCK), 0)
    lane_at = lax.broadcasted_iota(jnp.int32, (BLOCK, BLOCK), 1)
    unit = (row_at == lane_at).astype(jnp.float32)
    sub = lax.broadcasted_iota(jnp.int32, (BLOCK, 1), 0)
    for k in range(size // BLOCK):
        low = k * BLOCK
        work = jnp.concatenate([left[low:low + BLOCK, low:low + BLOCK], unit], axis=1)
        for j in range(BLOCK):
            pivot = work[j:j + 1, j:j + 1]
            scale = jnp.where(sub > j, work[:, j:j + 1] * (1.0 / pivot), 0.0)
            work = work - scale * work[j:j + 1, :]
        diagonal = jnp.sum(work[:, :BLOCK] * unit, axis=1, keepdims=True)
        solver = work[:, BLOCK:] * (1.0 / jnp.sqrt(diagonal))
        upper = exact(solver, left[low:low + BLOCK, :], (((1,), (0,)), ((), ())))
        lower = exact(solver, right[low:low + BLOCK, :], (((1,), (0,)), ((), ())))
        keep = (
            lax.broadcasted_iota(jnp.int32, (BLOCK, size), 1)
            >= lax.broadcasted_iota(jnp.int32, (BLOCK, size), 0) + low
        )
        upper = jnp.where(keep, upper, 0.0)
        factor_ref[low:low + BLOCK, :] = upper
        inverse[low:low + BLOCK, :] = lower
        if low + BLOCK < size:
            edge = (low + BLOCK) // 128 * 128
            rest = upper[:, edge:]
            left[edge:, edge:] = left[edge:, edge:] - exact(rest, rest, (((0,), (0,)), ((), ())))
            right[edge:, :] = right[edge:, :] - exact(rest, lower, (((0,), (0,)), ((), ())))
    solved = split(inverse[...])
    for e in range(rows_ref.shape[0]):
        bands_ref[0, 0, e] = product(split(rows_ref[e]), solved, ((1,), (1,)))


def orthonormalise(gram, rows, row_total):
    size = gram.shape[0]
    vmem = pl.BlockSpec(memory_space=pltpu.VMEM)
    return pl.pallas_call(
        functools.partial(factor_kernel, row_total),
        out_shape=(
            jax.ShapeDtypeStruct((1, 1) + rows.shape, jnp.float32),
            jax.ShapeDtypeStruct((size, size), jnp.float32),
        ),
        in_specs=[vmem, vmem],
        out_specs=(vmem, vmem),
        scratch_shapes=[pltpu.VMEM((size, size), jnp.float32)] * 3,
        name="factor",
    )(gram, rows)


def per_device(sizes, panel, tiles, codes):
    halo = exchange_halo(panel, sizes)
    rows, gram = apply_filter(codes, panel, tiles, halo, sizes)
    summed = sum_gram(gram, sizes)
    row_total = rows.shape[0] * rows.shape[1] * sizes[0] * sizes[1] * sizes[2]
    return orthonormalise(summed, rows, float(row_total))


def solution(mesh):
    in_specs = (
        P("gx", "gy", "gz", None, None),
        P("gx", "gy", "gz", None, None, None),
        P("gx", "gy", "gz", None),
    )
    out_specs = (P("gx", "gy", "gz", None, None), P())
    sizes = tuple(mesh.shape[a] for a in ("gx", "gy", "gz"))
    return jax.shard_map(
        functools.partial(per_device, sizes),
        mesh=mesh, in_specs=in_specs, out_specs=out_specs, check_vma=False,
    )
```

```python
import functools
import jax
import jax.numpy as jnp
from jax import lax
from jax.experimental import pallas as pl
from jax.experimental.pallas import tpu as pltpu
from jax.sharding import PartitionSpec as P

MESH = pl.DeviceIdType.MESH
PIECES = 4
BLOCK = 64
GROUP = 16


def split(value):
    high = value.astype(jnp.bfloat16)
    low = (value - high.astype(jnp.float32)).astype(jnp.bfloat16)
    return high, low


def product(left, right, dims):
    dot = functools.partial(
        lax.dot_general, dimension_numbers=(dims, ((), ())), preferred_element_type=jnp.float32
    )
    return dot(left[0], right[0]) + (dot(left[0], right[1]) + dot(left[1], right[0]))


def filter_kernel(sizes, codes_ref, panel_ref, tiles_ref, rows_ref, out_ref,
                  halo_ref, own_ref, tile_ref, high, low, tile_high, tile_low, gram_ref,
                  own_sem, tile_sem, x_sent, z_sent, y_sent, arrived, *sum_refs):
    nx, ny, nz = sizes
    ix, iy, iz = (lax.axis_index(a) for a in ("gx", "gy", "gz"))
    depth, rows = panel_ref.shape[2], panel_ref.shape[3]
    part = rows // PIECES
    slots, reach = tiles_ref.shape[3], depth + 2
    empty = 9 * reach
    squared = nx == 4
    below, above = iz > 0, iz < nz - 1
    front, back = iy > 0, iy < ny - 1

    if squared:
        across = ix + 1 - 2 * lax.rem(ix, 2)
        beside = lax.rem(ix + 2, 4)
        slot_a, valid_a = 2 * lax.rem(ix + 1, 2), None
        slot_b, valid_b = 2 - slot_a, (ix == 1) | (ix == 2)
        relays = (ix == 0) | (ix == 3)
    else:
        slot_a, valid_a = jnp.int32(0), ix > 0
        slot_b, valid_b = jnp.int32(2), ix < nx - 1

    def when(cond, action):
        if cond is None:
            action()
        else:
            pl.when(cond)(action)

    def both(*conds):
        conds = [c for c in conds if c is not None]
        return functools.reduce(jnp.logical_and, conds) if conds else None

    own_copy = pltpu.make_async_copy(panel_ref.at[0, 0], own_ref, own_sem)
    own_copy.start()
    tile_copies = [
        pltpu.make_async_copy(tiles_ref.at[0, 0, e], tile_ref.at[e], tile_sem.at[e])
        for e in range(depth)
    ]
    for tile_copy in tile_copies:
        tile_copy.start()

    barrier = pltpu.get_barrier_semaphore()
    peers = {
        axis: [lax.rem(at + d, n) for d in range(1, n)]
        for axis, at, n in (("gx", ix, nx), ("gy", iy, ny), ("gz", iz, nz))
    }
    for axis, group in peers.items():
        for peer in group:
            pl.semaphore_signal(barrier, inc=1, device_id={axis: peer}, device_id_type=MESH)
    pl.semaphore_wait(barrier, nx + ny + nz - 3)

    sends = []

    def own(z, c):
        return panel_ref.at[0, 0, z, pl.ds(c * part, part)]

    def cell(a, b, z, c):
        return halo_ref.at[a, b, z, pl.ds(c * part, part)]

    def send(cond, source, target, sem, slot, axis, device):
        a, b, z, c = slot

        def start():
            pltpu.make_async_remote_copy(
                src_ref=source,
                dst_ref=target,
                send_sem=sem,
                recv_sem=arrived.at[a, b, z, c],
                device_id={axis: device},
                device_id_type=MESH,
            ).start()

        when(cond, start)
        sends.append((cond, source, sem))

    def wait(cond, a, b, z, c):
        ref = cell(a, b, z, c)
        when(cond, lambda: pltpu.make_async_copy(ref, ref, arrived.at[a, b, z, c]).wait())

    def send_y(cond, source, a, z, c):
        send(both(cond, front), source, cell(a, 2, z, c), y_sent.at[0, a, z, c],
             (a, 2, z, c), "gy", iy - 1)
        send(both(cond, back), source, cell(a, 0, z, c), y_sent.at[1, a, z, c],
             (a, 0, z, c), "gy", iy + 1)

    def send_z(cond, source, a, z, c):
        if z == 0:
            send(both(cond, below), source, cell(a, 1, depth + 1, c), z_sent.at[0, a, c],
                 (a, 1, depth + 1, c), "gz", iz - 1)
        if z == depth - 1:
            send(both(cond, above), source, cell(a, 1, 0, c), z_sent.at[1, a, c],
                 (a, 1, 0, c), "gz", iz + 1)

    order = [0, depth - 1] + list(range(1, depth - 1)) if depth > 1 else [0]
    for z in order:
        for c in range(PIECES):
            if squared:
                target = 2 * lax.rem(ix, 2)
                send(None, own(z, c), cell(target, 1, z + 1, c), x_sent.at[0, z, c],
                     (target, 1, z + 1, c), "gx", across)
            else:
                send(valid_a, own(z, c), cell(2, 1, z + 1, c), x_sent.at[0, z, c],
                     (2, 1, z + 1, c), "gx", ix - 1)
                send(valid_b, own(z, c), cell(0, 1, z + 1, c), x_sent.at[1, z, c],
                     (0, 1, z + 1, c), "gx", ix + 1)
            send_z(None, own(z, c), 1, z, c)
    for z in order:
        for c in range(PIECES):
            send_y(None, own(z, c), 1, z + 1, c)

    def arrive(cond, a, z, c, relay=False):
        wait(cond, a, 1, z + 1, c)
        if relay and squared:
            target = 2 - a
            send(relays, cell(a, 1, z + 1, c), cell(target, 1, z + 1, c), x_sent.at[1, z, c],
                 (target, 1, z + 1, c), "gx", beside)
        send_z(cond, cell(a, 1, z + 1, c), a, z, c)
        send_y(cond, cell(a, 1, z + 1, c), a, z + 1, c)

    def arrive_z(cond, a):
        for side, slot in ((below, 0), (above, depth + 1)):
            for c in range(PIECES):
                ok = both(cond, side)
                wait(ok, a, 1, slot, c)
                send_y(ok, cell(a, 1, slot, c), a, slot, c)

    def place(a, b, z):
        return (a * 3 + b) * reach + z

    def keep(cond, a, b, z):
        def act():
            high[place(a, b, z)], low[place(a, b, z)] = split(halo_ref[a, b, z])

        when(cond, act)

    def take_y(cond, a, z):
        edge = below if z == 0 else above if z == depth + 1 else None
        for b, side in ((0, front), (2, back)):
            ok = both(cond, edge, side)
            for c in range(PIECES):
                wait(ok, a, b, z, c)
            keep(ok, a, b, z)

    def keep_z(cond, a):
        keep(both(cond, below), a, 1, 0)
        keep(both(cond, above), a, 1, depth + 1)

    def take_y_z(cond, a):
        take_y(cond, a, 0)
        take_y(cond, a, depth + 1)

    steps = [(k, c) for k in order for c in range(PIECES)]
    last = len(steps)
    work = [[] for _ in range(last + 1)]

    def later(step, action, *args):
        work[min(step, last)].append((action, args))

    def keep_own(z):
        if z == 0:
            own_copy.wait()
        high[place(1, 1, z + 1)], low[place(1, 1, z + 1)] = split(own_ref[z])

    def keep_tiles(e, begin, end):
        if begin == 0:
            tile_copies[e].wait()

        def body(s, carry):
            tile_high[e * slots + s], tile_low[e * slots + s] = split(tile_ref[e, s])
            return carry

        lax.fori_loop(begin, end, body, 0)

    cuts = list(range(0, slots, 3)) + [slots]
    chunks = [(e, p, q) for e in range(depth) for p, q in zip(cuts[:-1], cuts[1:])]
    for at, chunk in enumerate(chunks):
        later(1 + at * max(last - 3, 1) // len(chunks), keep_tiles, *chunk)
    for at, z in enumerate(order):
        later(at, keep_own, at)
        later((at + 2) * PIECES // 2, take_y, None, 1, z + 1)
        later((at + 1) * PIECES - 1, keep, valid_a, slot_a, 1, z + 1)
        later((at + 1) * PIECES, keep, valid_b, slot_b, 1, z + 1)
        later((at + 1) * PIECES + 2, take_y, valid_a, slot_a, z + 1)
        later((at + 1) * PIECES + 3, take_y, valid_b, slot_b, z + 1)
    half = last // 2
    high[empty] = jnp.zeros(high.shape[1:], high.dtype)
    low[empty] = jnp.zeros(low.shape[1:], low.dtype)
    for at in range(last + 1):
        if at < last:
            arrive(valid_a, slot_a, *steps[at], relay=True)
        if at >= 1:
            arrive(valid_b, slot_b, *steps[at - 1])
        if at == half:
            arrive_z(None, 1)
            keep_z(None, 1)
            later(half + 3, take_y_z, None, 1)
        if at == last - 2:
            arrive_z(valid_a, slot_a)
            keep_z(valid_a, slot_a)
            later(last, take_y_z, valid_a, slot_a)
        if at == last - 1:
            arrive_z(valid_b, slot_b)
            keep_z(valid_b, slot_b)
            later(last, take_y_z, valid_b, slot_b)
        for action, args in work[at]:
            action(*args)

    for e in range(depth):
        def apply(s, total, e=e):
            code = codes_ref[0, 0, e, s]
            a, b, z = code // 9, lax.rem(code // 3, 3), e + lax.rem(code, 3)
            x_at, y_at, z_at = ix + a - 1, iy + b - 1, iz * depth + z - 1
            inside = ((x_at >= 0) & (x_at < nx) & (y_at >= 0) & (y_at < ny)
                      & (z_at >= 0) & (z_at < nz * depth))
            at = jnp.where(inside, place(a, b, z), empty)
            tile = e * slots + s
            return total + product(
                (tile_high[tile], tile_low[tile]), (high[at], low[at]), ((1,), (0,))
            )

        filtered = lax.fori_loop(0, slots, apply, -0.5 * own_ref[e], unroll=2)
        rows_ref[e] = filtered
        pieces = split(filtered)
        term = product(pieces, pieces, ((0,), (0,)))
        gram_ref[...] = term if e == 0 else gram_ref[...] + term
    sum_over_mesh(sizes, peers, gram_ref, out_ref, *sum_refs)
    for cond, source, sem in sends:
        when(cond, lambda source=source, sem=sem: pltpu.make_async_copy(source, source, sem).wait())


def sum_over_mesh(sizes, peers, gram_ref, out_ref, from_y, part_y, from_x, from_z, full,
                  y_send, y_recv, x_send, x_recv, z_send, z_recv,
               gx_send, gx_recv, gy_send, gy_recv):
    nx, ny, nz = sizes
    ix, iy, iz = (lax.axis_index(a) for a in ("gx", "gy", "gz"))
    rows_y = gram_ref.shape[0] // ny
    rows_x = rows_y // nx
    def copy(source, target, send_sem, recv_sem, axis, peer):
        remote = pltpu.make_async_remote_copy(
            src_ref=source, dst_ref=target, send_sem=send_sem, recv_sem=recv_sem,
            device_id={axis: peer}, device_id_type=MESH,
        )
        remote.start()
        return remote

    def finish(copies):
        for remote in copies:
            remote.wait()

    def block(ref, at, count):
        return ref.at[pl.ds(pl.multiple_of(at * count, count), count)]

    finish([
        copy(block(gram_ref, peer, rows_y), from_y.at[d], y_send.at[d], y_recv.at[d], "gy", peer)
        for d, peer in enumerate(peers["gy"])
    ])
    total = gram_ref[pl.ds(pl.multiple_of(iy * rows_y, rows_y), rows_y), :]
    for d in range(ny - 1):
        total = total + from_y[d]
    part_y[...] = total
    finish([
        copy(block(part_y, peer, rows_x), from_x.at[d], x_send.at[d], x_recv.at[d], "gx", peer)
        for d, peer in enumerate(peers["gx"])
    ])
    total = part_y[pl.ds(pl.multiple_of(ix * rows_x, rows_x), rows_x), :]
    for d in range(nx - 1):
        total = total + from_x[d]
    from_z[pl.ds(iz, 1)] = total[None]
    started = [
        copy(from_z.at[iz], from_z.at[iz], z_send.at[d], z_recv.at[iz], "gz", peer)
        for d, peer in enumerate(peers["gz"])
    ]
    for remote in started:
        remote.wait_send()
    for peer in peers["gz"]:
        ref = from_z.at[peer]
        pltpu.make_async_copy(ref, ref, z_recv.at[peer]).wait()
    total = from_z[0]
    for d in range(1, nz):
        total = total + from_z[d]
    mine = iy * nx + ix
    full[pl.ds(pl.multiple_of(mine * rows_x, rows_x), rows_x), :] = total
    started = [
        copy(block(full, mine, rows_x), block(full, mine, rows_x), gx_send.at[d], gx_recv.at[ix],
             "gx", peer)
        for d, peer in enumerate(peers["gx"])
    ]
    for remote in started:
        remote.wait_send()
    for peer in peers["gx"]:
        ref = block(full, iy * nx + peer, rows_x)
        pltpu.make_async_copy(ref, ref, gx_recv.at[peer]).wait()
    started = [
        copy(block(full, iy, rows_y), block(full, iy, rows_y), gy_send.at[d], gy_recv.at[iy],
             "gy", peer)
        for d, peer in enumerate(peers["gy"])
    ]
    for remote in started:
        remote.wait_send()
    for peer in peers["gy"]:
        ref = block(full, peer, rows_y)
        pltpu.make_async_copy(ref, ref, gy_recv.at[peer]).wait()
    out_ref[...] = full[...]


def filter_and_gram(codes, panel, tiles, sizes):
    nx, ny, nz = sizes
    depth, slots, rows, width = tiles.shape[2], tiles.shape[3], panel.shape[3], panel.shape[4]
    reach = depth + 2
    rows_y = width // ny
    rows_x = rows_y // nx
    hbm = pl.BlockSpec(memory_space=pl.ANY)
    vmem = pl.BlockSpec(memory_space=pltpu.VMEM)
    dma = pltpu.SemaphoreType.DMA
    half = jnp.bfloat16
    return pl.pallas_call(
        functools.partial(filter_kernel, sizes),
        out_shape=(
            jax.ShapeDtypeStruct((depth, rows, width), jnp.float32),
            jax.ShapeDtypeStruct((width, width), jnp.float32),
        ),
        in_specs=[pl.BlockSpec(memory_space=pltpu.SMEM), hbm, hbm],
        out_specs=(vmem, vmem),
        scratch_shapes=[
            pltpu.VMEM((3, 3, reach, rows, width), jnp.float32),
            pltpu.VMEM((depth, rows, width), jnp.float32),
            pltpu.VMEM((depth, slots, rows, rows), jnp.float32),
            pltpu.VMEM((9 * reach + 1, rows, width), half),
            pltpu.VMEM((9 * reach + 1, rows, width), half),
            pltpu.VMEM((depth * slots, rows, rows), half),
            pltpu.VMEM((depth * slots, rows, rows), half),
            pltpu.VMEM((width, width), jnp.float32),
            dma,
            dma((depth,)),
            dma((2, depth, PIECES)),
            dma((2, 3, PIECES)),
            dma((2, 3, reach, PIECES)),
            dma((3, 3, reach, PIECES)),
            pltpu.VMEM((max(ny - 1, 1), rows_y, width), jnp.float32),
            pltpu.VMEM((rows_y, width), jnp.float32),
            pltpu.VMEM((max(nx - 1, 1), rows_x, width), jnp.float32),
            pltpu.VMEM((nz, rows_x, width), jnp.float32),
            pltpu.VMEM((width, width), jnp.float32),
            dma((ny,)), dma((ny,)), dma((nx,)), dma((nx,)), dma((nz,)), dma((nz,)),
            dma((nx,)), dma((nx,)), dma((ny,)), dma((ny,)),
        ],
        compiler_params=pltpu.CompilerParams(
            collective_id=0, has_side_effects=True, vmem_limit_bytes=61 << 20
        ),
        name="filter",
    )(codes, panel, tiles)


def factor_kernel(row_total, gram_ref, rows_ref, bands_ref, factor_ref, left, right, inverse):
    size = gram_ref.shape[0]
    exact = functools.partial(
        lax.dot_general, preferred_element_type=jnp.float32, precision=lax.Precision.HIGHEST
    )
    left[...] = gram_ref[...] / row_total
    right[...] = (
        lax.broadcasted_iota(jnp.int32, (size, size), 0)
        == lax.broadcasted_iota(jnp.int32, (size, size), 1)
    ).astype(jnp.float32)
    row_at = lax.broadcasted_iota(jnp.int32, (BLOCK, BLOCK), 0)
    lane_at = lax.broadcasted_iota(jnp.int32, (BLOCK, BLOCK), 1)
    unit = (row_at == lane_at).astype(jnp.float32)
    sub = lax.broadcasted_iota(jnp.int32, (BLOCK, 2 * BLOCK), 0)
    for k in range(size // BLOCK):
        low = k * BLOCK
        work = jnp.concatenate([left[low:low + BLOCK, low:low + BLOCK], unit], axis=1)
        for start in range(0, BLOCK, GROUP):
            columns = [
                jnp.broadcast_to(work[:, j:j + 1], (BLOCK, 2 * BLOCK))
                for j in range(start, start + GROUP)
            ]
            for at in range(GROUP):
                j = start + at
                inverted = 1.0 / columns[at][j:j + 1, :]
                scale = jnp.where(sub > j, columns[at] * inverted, 0.0)
                for later in range(at + 1, GROUP):
                    columns[later] = columns[later] - scale * columns[later][j:j + 1, :]
                work = work - scale * work[j:j + 1, :]
        diagonal = jnp.sum(work[:, :BLOCK] * unit, axis=1, keepdims=True)
        solver = work[:, BLOCK:] * (1.0 / jnp.sqrt(diagonal))
        upper = exact(solver, left[low:low + BLOCK, :], (((1,), (0,)), ((), ())))
        lower = exact(solver, right[low:low + BLOCK, :], (((1,), (0,)), ((), ())))
        keep = (
            lax.broadcasted_iota(jnp.int32, (BLOCK, size), 1)
            >= lax.broadcasted_iota(jnp.int32, (BLOCK, size), 0) + low
        )
        upper = jnp.where(keep, upper, 0.0)
        factor_ref[low:low + BLOCK, :] = upper
        inverse[low:low + BLOCK, :] = lower
        if low + BLOCK < size:
            edge = (low + BLOCK) // 128 * 128
            rest = upper[:, edge:]
            left[edge:, edge:] = left[edge:, edge:] - exact(rest, rest, (((0,), (0,)), ((), ())))
            right[edge:, :] = right[edge:, :] - exact(rest, lower, (((0,), (0,)), ((), ())))
    solved = split(inverse[...])
    for e in range(rows_ref.shape[0]):
        bands_ref[0, 0, e] = product(split(rows_ref[e]), solved, ((1,), (1,)))


def orthonormalise(gram, rows, row_total):
    size = gram.shape[0]
    vmem = pl.BlockSpec(memory_space=pltpu.VMEM)
    return pl.pallas_call(
        functools.partial(factor_kernel, row_total),
        out_shape=(
            jax.ShapeDtypeStruct((1, 1) + rows.shape, jnp.float32),
            jax.ShapeDtypeStruct((size, size), jnp.float32),
        ),
        in_specs=[vmem, vmem],
        out_specs=(vmem, vmem),
        scratch_shapes=[pltpu.VMEM((size, size), jnp.float32)] * 3,
        name="factor",
    )(gram, rows)


def per_device(sizes, panel, tiles, codes):
    rows, summed = filter_and_gram(codes, panel, tiles, sizes)
    row_total = rows.shape[0] * rows.shape[1] * sizes[0] * sizes[1] * sizes[2]
    return orthonormalise(summed, rows, float(row_total))


def solution(mesh):
    in_specs = (
        P("gx", "gy", "gz", None, None),
        P("gx", "gy", "gz", None, None, None),
        P("gx", "gy", "gz", None),
    )
    out_specs = (P("gx", "gy", "gz", None, None), P())
    sizes = tuple(mesh.shape[a] for a in ("gx", "gy", "gz"))
    return jax.shard_map(
        functools.partial(per_device, sizes),
        mesh=mesh, in_specs=in_specs, out_specs=out_specs, check_vma=False,
    )
```

```python
import functools
import jax
import jax.numpy as jnp
from jax import lax
from jax.experimental import pallas as pl
from jax.experimental.pallas import tpu as pltpu
from jax.sharding import PartitionSpec as P

MESH = pl.DeviceIdType.MESH
PIECES = 4
BLOCK = 64
GROUP = 16


def split(value):
    high = value.astype(jnp.bfloat16)
    low = (value - high.astype(jnp.float32)).astype(jnp.bfloat16)
    return high, low


def product(left, right, dims):
    dot = functools.partial(
        lax.dot_general, dimension_numbers=(dims, ((), ())), preferred_element_type=jnp.float32
    )
    return dot(left[0], right[0]) + (dot(left[0], right[1]) + dot(left[1], right[0]))


def filter_kernel(sizes, codes_ref, panel_ref, tiles_ref, rows_ref, out_ref,
                  halo_ref, own_ref, tile_ref, high, low, tile_high, tile_low, gram_ref,
                  own_sem, tile_sem, x_sent, z_sent, y_sent, arrived, *sum_refs):
    nx, ny, nz = sizes
    ix, iy, iz = (lax.axis_index(a) for a in ("gx", "gy", "gz"))
    depth, rows = panel_ref.shape[2], panel_ref.shape[3]
    part = rows // PIECES
    slots, reach = tiles_ref.shape[3], depth + 2
    empty = 9 * reach
    squared = nx == 4
    below, above = iz > 0, iz < nz - 1
    front, back = iy > 0, iy < ny - 1

    if squared:
        across = ix + 1 - 2 * lax.rem(ix, 2)
        beside = lax.rem(ix + 2, 4)
        slot_a, valid_a = 2 * lax.rem(ix + 1, 2), None
        slot_b, valid_b = 2 - slot_a, (ix == 1) | (ix == 2)
        relays = (ix == 0) | (ix == 3)
    else:
        slot_a, valid_a = jnp.int32(0), ix > 0
        slot_b, valid_b = jnp.int32(2), ix < nx - 1

    def when(cond, action):
        if cond is None:
            action()
        else:
            pl.when(cond)(action)

    def both(*conds):
        conds = [c for c in conds if c is not None]
        return functools.reduce(jnp.logical_and, conds) if conds else None

    own_copy = pltpu.make_async_copy(panel_ref.at[0, 0], own_ref, own_sem)
    own_copy.start()
    tile_copies = [
        pltpu.make_async_copy(tiles_ref.at[0, 0, e], tile_ref.at[e], tile_sem.at[e])
        for e in range(depth)
    ]
    for tile_copy in tile_copies:
        tile_copy.start()

    barrier = pltpu.get_barrier_semaphore()
    peers = {
        axis: [lax.rem(at + d, n) for d in range(1, n)]
        for axis, at, n in (("gx", ix, nx), ("gy", iy, ny), ("gz", iz, nz))
    }
    for axis, group in peers.items():
        for peer in group:
            pl.semaphore_signal(barrier, inc=1, device_id={axis: peer}, device_id_type=MESH)
    pl.semaphore_wait(barrier, nx + ny + nz - 3)

    sends = []

    def own(z, c):
        return panel_ref.at[0, 0, z, pl.ds(c * part, part)]

    def cell(a, b, z, c):
        return halo_ref.at[a, b, z, pl.ds(c * part, part)]

    def send(cond, source, target, sem, slot, axis, device):
        a, b, z, c = slot

        def start():
            pltpu.make_async_remote_copy(
                src_ref=source,
                dst_ref=target,
                send_sem=sem,
                recv_sem=arrived.at[a, b, z, c],
                device_id={axis: device},
                device_id_type=MESH,
            ).start()

        when(cond, start)
        sends.append((cond, source, sem))

    def wait(cond, a, b, z, c):
        ref = cell(a, b, z, c)
        when(cond, lambda: pltpu.make_async_copy(ref, ref, arrived.at[a, b, z, c]).wait())

    def send_y(cond, source, a, z, c):
        send(both(cond, front), source, cell(a, 2, z, c), y_sent.at[0, a, z, c],
             (a, 2, z, c), "gy", iy - 1)
        send(both(cond, back), source, cell(a, 0, z, c), y_sent.at[1, a, z, c],
             (a, 0, z, c), "gy", iy + 1)

    def send_z(cond, source, a, z, c):
        if z == 0:
            send(both(cond, below), source, cell(a, 1, depth + 1, c), z_sent.at[0, a, c],
                 (a, 1, depth + 1, c), "gz", iz - 1)
        if z == depth - 1:
            send(both(cond, above), source, cell(a, 1, 0, c), z_sent.at[1, a, c],
                 (a, 1, 0, c), "gz", iz + 1)

    order = [0, depth - 1] + list(range(1, depth - 1)) if depth > 1 else [0]
    for z in order:
        for c in range(PIECES):
            if squared:
                target = 2 * lax.rem(ix, 2)
                send(None, own(z, c), cell(target, 1, z + 1, c), x_sent.at[0, z, c],
                     (target, 1, z + 1, c), "gx", across)
            else:
                send(valid_a, own(z, c), cell(2, 1, z + 1, c), x_sent.at[0, z, c],
                     (2, 1, z + 1, c), "gx", ix - 1)
                send(valid_b, own(z, c), cell(0, 1, z + 1, c), x_sent.at[1, z, c],
                     (0, 1, z + 1, c), "gx", ix + 1)
            send_z(None, own(z, c), 1, z, c)
    for z in order:
        for c in range(PIECES):
            send_y(None, own(z, c), 1, z + 1, c)

    def arrive(cond, a, z, c, relay=False):
        wait(cond, a, 1, z + 1, c)
        if relay and squared:
            target = 2 - a
            send(relays, cell(a, 1, z + 1, c), cell(target, 1, z + 1, c), x_sent.at[1, z, c],
                 (target, 1, z + 1, c), "gx", beside)
        send_z(cond, cell(a, 1, z + 1, c), a, z, c)
        send_y(cond, cell(a, 1, z + 1, c), a, z + 1, c)

    def arrive_z(cond, a):
        for side, slot in ((below, 0), (above, depth + 1)):
            for c in range(PIECES):
                ok = both(cond, side)
                wait(ok, a, 1, slot, c)
                send_y(ok, cell(a, 1, slot, c), a, slot, c)

    def place(a, b, z):
        return (a * 3 + b) * reach + z

    def keep(cond, a, b, z):
        def act():
            high[place(a, b, z)], low[place(a, b, z)] = split(halo_ref[a, b, z])

        when(cond, act)

    def take_y(cond, a, z):
        edge = below if z == 0 else above if z == depth + 1 else None
        for b, side in ((0, front), (2, back)):
            ok = both(cond, edge, side)
            for c in range(PIECES):
                wait(ok, a, b, z, c)
            keep(ok, a, b, z)

    def keep_z(cond, a):
        keep(both(cond, below), a, 1, 0)
        keep(both(cond, above), a, 1, depth + 1)

    def take_y_z(cond, a):
        take_y(cond, a, 0)
        take_y(cond, a, depth + 1)

    steps = [(k, c) for k in order for c in range(PIECES)]
    last = len(steps)
    work = [[] for _ in range(last + 1)]

    def later(step, action, *args):
        work[min(step, last)].append((action, args))

    def keep_own(z):
        if z == 0:
            own_copy.wait()
        high[place(1, 1, z + 1)], low[place(1, 1, z + 1)] = split(own_ref[z])

    def keep_tiles(e, begin, end):
        if begin == 0:
            tile_copies[e].wait()

        def body(s, carry):
            tile_high[e * slots + s], tile_low[e * slots + s] = split(tile_ref[e, s])
            return carry

        lax.fori_loop(begin, end, body, 0)

    cuts = list(range(0, slots, 3)) + [slots]
    chunks = [(e, p, q) for e in range(depth) for p, q in zip(cuts[:-1], cuts[1:])]
    for at, chunk in enumerate(chunks):
        later(1 + at * max(last - 3, 1) // len(chunks), keep_tiles, *chunk)
    for at, z in enumerate(order):
        later(at, keep_own, at)
        later((at + 2) * PIECES // 2, take_y, None, 1, z + 1)
        later((at + 1) * PIECES - 1, keep, valid_a, slot_a, 1, z + 1)
        later((at + 1) * PIECES, keep, valid_b, slot_b, 1, z + 1)
        later((at + 1) * PIECES + 2, take_y, valid_a, slot_a, z + 1)
        later((at + 1) * PIECES + 3, take_y, valid_b, slot_b, z + 1)
    half = last // 2
    high[empty] = jnp.zeros(high.shape[1:], high.dtype)
    low[empty] = jnp.zeros(low.shape[1:], low.dtype)
    for at in range(last + 1):
        if at < last:
            arrive(valid_a, slot_a, *steps[at], relay=True)
        if at >= 1:
            arrive(valid_b, slot_b, *steps[at - 1])
        if at == half:
            arrive_z(None, 1)
            keep_z(None, 1)
            later(half + 3, take_y_z, None, 1)
        if at == last - 2:
            arrive_z(valid_a, slot_a)
            keep_z(valid_a, slot_a)
            later(last, take_y_z, valid_a, slot_a)
        if at == last - 1:
            arrive_z(valid_b, slot_b)
            keep_z(valid_b, slot_b)
            later(last, take_y_z, valid_b, slot_b)
        for action, args in work[at]:
            action(*args)

    highs, lows = [], []
    for e in range(depth):
        left, right = [], []
        for slot in range(slots):
            code = codes_ref[0, 0, e, slot]
            a, b, z = code // 9, lax.rem(code // 3, 3), e + lax.rem(code, 3)
            x_at, y_at, z_at = ix + a - 1, iy + b - 1, iz * depth + z - 1
            inside = ((x_at >= 0) & (x_at < nx) & (y_at >= 0) & (y_at < ny)
                      & (z_at >= 0) & (z_at < nz * depth))
            at = jnp.where(inside, place(a, b, z), empty)
            tile = e * slots + slot
            left += [tile_high[tile], tile_low[tile], tile_high[tile]]
            right += [high[at], high[at], low[at]]
        filtered = -0.5 * own_ref[e] + lax.dot_general(
            jnp.concatenate(left, axis=1), jnp.concatenate(right, axis=0),
            (((1,), (0,)), ((), ())), preferred_element_type=jnp.float32,
        )
        rows_ref[e] = filtered
        pieces = split(filtered)
        highs.append(pieces[0])
        lows.append(pieces[1])
    tall = functools.partial(
        lax.dot_general, dimension_numbers=(((0,), (0,)), ((), ())),
        preferred_element_type=jnp.float32,
    )
    whole_high = jnp.concatenate(highs, axis=0)
    mixed = tall(whole_high, jnp.concatenate(lows, axis=0))
    gram = tall(whole_high, whole_high) + mixed + mixed.T
    for part_at, (rows_at, lanes_at) in enumerate(gram_parts(sizes, gram.shape[0])):
        gram_ref[part_at] = gram[rows_at:rows_at + gram_ref.shape[1], lanes_at:lanes_at + 128]
    sum_over_mesh(sizes, peers, gram_ref, out_ref, *sum_refs)
    for cond, source, sem in sends:
        when(cond, lambda source=source, sem=sem: pltpu.make_async_copy(source, source, sem).wait())


def gram_parts(sizes, size):
    half = size // 2
    folded = half % 128 == 0 and half % (sizes[0] * sizes[1] * 8) == 0
    lanes = range(0, size, 128)
    if not folded:
        return [(0, lane) for lane in lanes]
    return [(0, lane) for lane in lanes] + [(half, lane) for lane in lanes if lane >= half]


def part_rows(sizes, size):
    return size // 2 if gram_parts(sizes, size)[-1][0] else size


def sum_over_mesh(sizes, peers, gram_ref, out_ref, from_y, part_y, from_x, from_z, full,
                  y_send, y_recv, x_send, x_recv, z_send, z_recv,
                  gx_send, gx_recv, gy_send, gy_recv):
    nx, ny, nz = sizes
    ix, iy, iz = (lax.axis_index(a) for a in ("gx", "gy", "gz"))
    count, rows = gram_ref.shape[:2]
    rows_y = rows // ny
    rows_x = rows_y // nx
    mine = iy * nx + ix

    def copy(source, target, send_sem, recv_sem, axis, peer):
        remote = pltpu.make_async_remote_copy(
            src_ref=source, dst_ref=target, send_sem=send_sem, recv_sem=recv_sem,
            device_id={axis: peer}, device_id_type=MESH,
        )
        remote.start()
        return remote

    def window(at, size):
        return pl.ds(pl.multiple_of(at * size, size), size)

    def landed(started, group, ref_of, sems, p):
        for remote in started:
            remote.wait_send()
        for peer in group:
            ref = ref_of(peer)
            pltpu.make_async_copy(ref, ref, sems.at[peer, p]).wait()

    def start_y(p, started):
        return [
            copy(gram_ref.at[p, window(peer, rows_y)], from_y.at[d, p],
                 y_send.at[d, p], y_recv.at[d, p], "gy", peer)
            for d, peer in enumerate(peers["gy"])
        ]

    def start_x(p, started):
        for remote in started:
            remote.wait()
        total = gram_ref[p, window(iy, rows_y), :]
        for d in range(ny - 1):
            total = total + from_y[d, p]
        part_y[p] = total
        return [
            copy(part_y.at[p, window(peer, rows_x)], from_x.at[d, p],
                 x_send.at[d, p], x_recv.at[d, p], "gx", peer)
            for d, peer in enumerate(peers["gx"])
        ]

    def start_z(p, started):
        for remote in started:
            remote.wait()
        total = part_y[p, window(ix, rows_x), :]
        for d in range(nx - 1):
            total = total + from_x[d, p]
        from_z[iz, p] = total
        return [
            copy(from_z.at[iz, p], from_z.at[iz, p], z_send.at[d, p], z_recv.at[iz, p],
                 "gz", peer)
            for d, peer in enumerate(peers["gz"])
        ]

    def gather_x(p, started):
        landed(started, peers["gz"], lambda peer: from_z.at[peer, p], z_recv, p)
        total = from_z[0, p]
        for d in range(1, nz):
            total = total + from_z[d, p]
        full[p, window(mine, rows_x), :] = total
        ref = full.at[p, window(mine, rows_x)]
        return [
            copy(ref, ref, gx_send.at[d, p], gx_recv.at[ix, p], "gx", peer)
            for d, peer in enumerate(peers["gx"])
        ]

    def gather_y(p, started):
        landed(started, peers["gx"],
               lambda peer: full.at[p, window(iy * nx + peer, rows_x)], gx_recv, p)
        ref = full.at[p, window(iy, rows_y)]
        return [
            copy(ref, ref, gy_send.at[d, p], gy_recv.at[iy, p], "gy", peer)
            for d, peer in enumerate(peers["gy"])
        ]

    started = [None] * count
    for phase in (start_y, start_x, start_z, gather_x, gather_y):
        for p in range(count):
            started[p] = phase(p, started[p])
    size = out_ref.shape[0]
    corners = gram_parts(sizes, size)
    if rows < size:
        out_ref[rows:, :rows] = jnp.zeros((size - rows, rows), out_ref.dtype)
    for p in range(count):
        landed(started[p], peers["gy"], lambda peer: full.at[p, window(peer, rows_y)], gy_recv, p)
        row, lane = corners[p]
        out_ref[row:row + rows, lane:lane + 128] = full[p]


def filter_and_gram(codes, panel, tiles, sizes):
    nx, ny, nz = sizes
    depth, slots, rows, width = tiles.shape[2], tiles.shape[3], panel.shape[3], panel.shape[4]
    reach = depth + 2
    parts = len(gram_parts(sizes, width))
    gram_rows = part_rows(sizes, width)
    rows_y = gram_rows // ny
    rows_x = rows_y // nx
    hbm = pl.BlockSpec(memory_space=pl.ANY)
    vmem = pl.BlockSpec(memory_space=pltpu.VMEM)
    dma = pltpu.SemaphoreType.DMA
    half = jnp.bfloat16
    return pl.pallas_call(
        functools.partial(filter_kernel, sizes),
        out_shape=(
            jax.ShapeDtypeStruct((depth, rows, width), jnp.float32),
            jax.ShapeDtypeStruct((width, width), jnp.float32),
        ),
        in_specs=[pl.BlockSpec(memory_space=pltpu.SMEM), hbm, hbm],
        out_specs=(vmem, vmem),
        scratch_shapes=[
            pltpu.VMEM((3, 3, reach, rows, width), jnp.float32),
            pltpu.VMEM((depth, rows, width), jnp.float32),
            pltpu.VMEM((depth, slots, rows, rows), jnp.float32),
            pltpu.VMEM((9 * reach + 1, rows, width), half),
            pltpu.VMEM((9 * reach + 1, rows, width), half),
            pltpu.VMEM((depth * slots, rows, rows), half),
            pltpu.VMEM((depth * slots, rows, rows), half),
            pltpu.VMEM((parts, gram_rows, 128), jnp.float32),
            dma,
            dma((depth,)),
            dma((2, depth, PIECES)),
            dma((2, 3, PIECES)),
            dma((2, 3, reach, PIECES)),
            dma((3, 3, reach, PIECES)),
            pltpu.VMEM((max(ny - 1, 1), parts, rows_y, 128), jnp.float32),
            pltpu.VMEM((parts, rows_y, 128), jnp.float32),
            pltpu.VMEM((max(nx - 1, 1), parts, rows_x, 128), jnp.float32),
            pltpu.VMEM((nz, parts, rows_x, 128), jnp.float32),
            pltpu.VMEM((parts, gram_rows, 128), jnp.float32),
            *[dma((n, parts)) for n in (ny, ny, nx, nx, nz, nz, nx, nx, ny, ny)],
        ],
        compiler_params=pltpu.CompilerParams(
            collective_id=0, has_side_effects=True, vmem_limit_bytes=61 << 20
        ),
        name="filter",
    )(codes, panel, tiles)


def factor_kernel(row_total, gram_ref, rows_ref, bands_ref, factor_ref, left, right, inverse):
    size = gram_ref.shape[0]
    exact = functools.partial(
        lax.dot_general, preferred_element_type=jnp.float32, precision=lax.Precision.HIGHEST
    )
    left[...] = gram_ref[...] / row_total
    right[...] = (
        lax.broadcasted_iota(jnp.int32, (size, size), 0)
        == lax.broadcasted_iota(jnp.int32, (size, size), 1)
    ).astype(jnp.float32)
    row_at = lax.broadcasted_iota(jnp.int32, (BLOCK, BLOCK), 0)
    lane_at = lax.broadcasted_iota(jnp.int32, (BLOCK, BLOCK), 1)
    unit = (row_at == lane_at).astype(jnp.float32)
    sub = lax.broadcasted_iota(jnp.int32, (BLOCK, 2 * BLOCK), 0)
    for k in range(size // BLOCK):
        low = k * BLOCK
        work = jnp.concatenate([left[low:low + BLOCK, low:low + BLOCK], unit], axis=1)
        for start in range(0, BLOCK, GROUP):
            columns = [
                jnp.broadcast_to(work[:, j:j + 1], (BLOCK, 2 * BLOCK))
                for j in range(start, start + GROUP)
            ]
            for at in range(GROUP):
                j = start + at
                inverted = 1.0 / columns[at][j:j + 1, :]
                scale = jnp.where(sub > j, columns[at] * inverted, 0.0)
                for later in range(at + 1, GROUP):
                    columns[later] = columns[later] - scale * columns[later][j:j + 1, :]
                work = work - scale * work[j:j + 1, :]
        diagonal = jnp.sum(work[:, :BLOCK] * unit, axis=1, keepdims=True)
        solver = work[:, BLOCK:] * (1.0 / jnp.sqrt(diagonal))
        upper = exact(solver, left[low:low + BLOCK, :], (((1,), (0,)), ((), ())))
        lower = exact(solver, right[low:low + BLOCK, :], (((1,), (0,)), ((), ())))
        keep = (
            lax.broadcasted_iota(jnp.int32, (BLOCK, size), 1)
            >= lax.broadcasted_iota(jnp.int32, (BLOCK, size), 0) + low
        )
        upper = jnp.where(keep, upper, 0.0)
        factor_ref[low:low + BLOCK, :] = upper
        inverse[low:low + BLOCK, :] = lower
        if low + BLOCK < size:
            edge = (low + BLOCK) // 128 * 128
            rest = upper[:, edge:]
            left[edge:, edge:] = left[edge:, edge:] - exact(rest, rest, (((0,), (0,)), ((), ())))
            right[edge:, :] = right[edge:, :] - exact(rest, lower, (((0,), (0,)), ((), ())))
    solved = split(inverse[...])
    for e in range(rows_ref.shape[0]):
        bands_ref[0, 0, e] = product(split(rows_ref[e]), solved, ((1,), (1,)))


def orthonormalise(gram, rows, row_total):
    size = gram.shape[0]
    vmem = pl.BlockSpec(memory_space=pltpu.VMEM)
    return pl.pallas_call(
        functools.partial(factor_kernel, row_total),
        out_shape=(
            jax.ShapeDtypeStruct((1, 1) + rows.shape, jnp.float32),
            jax.ShapeDtypeStruct((size, size), jnp.float32),
        ),
        in_specs=[vmem, vmem],
        out_specs=(vmem, vmem),
        scratch_shapes=[pltpu.VMEM((size, size), jnp.float32)] * 3,
        name="factor",
    )(gram, rows)


def per_device(sizes, panel, tiles, codes):
    rows, summed = filter_and_gram(codes, panel, tiles, sizes)
    row_total = rows.shape[0] * rows.shape[1] * sizes[0] * sizes[1] * sizes[2]
    return orthonormalise(summed, rows, float(row_total))


def solution(mesh):
    in_specs = (
        P("gx", "gy", "gz", None, None),
        P("gx", "gy", "gz", None, None, None),
        P("gx", "gy", "gz", None),
    )
    out_specs = (P("gx", "gy", "gz", None, None), P())
    sizes = tuple(mesh.shape[a] for a in ("gx", "gy", "gz"))
    return jax.shard_map(
        functools.partial(per_device, sizes),
        mesh=mesh, in_specs=in_specs, out_specs=out_specs, check_vma=False,
    )
```
